32 devices in a mesh: tp: 8 (over y, x, core), sp: 4 (over z).
Axes of the slice: x: 2, y: 2, z: 4, core: 2. Of those that a mesh axis runs over, the one named last changes fastest.
Arguments:
- tokens: bfloat16 [4, 4096, 1024], P('sp', 'tp'), may hold values from -6 to 6
- lengths: int32 [4], P('sp'), may hold values from 1024 to 4096, as said below
- w_qkv: bfloat16 [3, 1024, 1024], P(None, 'sp', 'tp'), may hold values from -0.1875 to 0.1875
- w_out: bfloat16 [1024, 1024], P('tp', 'sp'), may hold values from -0.75 to 0.75
- w_fc: bfloat16 [1024, 4096], P('sp', 'tp'), may hold values from -0.1875 to 0.1875
- w_proj: bfloat16 [4096, 1024], P('tp', 'sp'), may hold values from -0.09375 to 0.09375
- norm_gain: float32 [2, 1024], P(None, ('tp', 'sp')), may hold values from 0.1 to 1.9
- norm_bias: float32 [2, 1024], P(None, ('tp', 'sp')), may hold values from -3 to 3
- cotangent: bfloat16 [4, 4096, 1024], P('sp', 'tp'), may hold values from -6 to 6
Outputs:
- result: bfloat16 [4, 4096, 1024], P('sp', 'tp')
- grad_tokens: bfloat16 [4, 4096, 1024], P('sp', 'tp')
- grad_qkv: float32 [3, 1024, 1024], P(None, 'sp', 'tp')
- grad_out: float32 [1024, 1024], P('tp', 'sp')
- grad_fc: float32 [1024, 4096], P('sp', 'tp')
- grad_proj: float32 [4096, 1024], P('tp', 'sp')
- grad_gain: float32 [2, 1024], P(None, ('tp', 'sp'))
- grad_bias: float32 [2, 1024], P(None, ('tp', 'sp'))
The draws below stay inside these ranges and needn't reach their ends.
Inputs may be any that keep to these rules, and one draw needn't show every extreme that they name: lengths[s] counts the valid leading positions of window s; the rest is padding; some window is full.
All inputs are finite; a program needn't handle non-finite values.
Results may differ from the reference program's by a relative error of at most 0.022.
Values may be sent and summed in bfloat16 or wider, within the bound.
No kernel may reach another device: no remote copies, remote signals or barrier semaphores. Data moves between devices by JAX's collectives and lax.ppermute only.
A program may use at most 256 MiB of HBM per device.

```python
import jax
import jax.numpy as jnp
from jax import lax

HEADS = 16
HEAD = 64
FF = 4096
BLOCK = 128
D = 1024
WIN = 4096
SEQS = 4


def draw_lengths(key, part):
    low_len = max(WIN // 4, BLOCK)
    values = jax.random.randint(jax.random.fold_in(key, 11), (SEQS,), low_len, WIN + 1)
    longest = jax.random.randint(jax.random.fold_in(key, 12), (), 0, SEQS)
    return jnp.where(jnp.arange(SEQS) == longest, WIN, values).astype(jnp.int32)


def shard_levels(rng, extent, pieces, smallest, largest):
    loudness, own = 1.0, jax.random.fold_in(rng, 6)
    for axis_at, shards_of in pieces:
        draws = jnp.exp(jax.random.uniform(jax.random.fold_in(own, axis_at), (shards_of,), jnp.float32, smallest / len(pieces), largest / len(pieces)))
        loudness = loudness * jnp.repeat(draws, extent[axis_at] // shards_of).reshape([-1 if axis == axis_at else 1 for axis in range(len(extent))])
    return loudness


def centred(rng, extent, width, most, shards=(), kind=jnp.bfloat16):
    array = jax.random.normal(rng, extent, jnp.float32) * width
    if len(shards) > 0:
        array = shard_levels(rng, extent, shards, -0.22, 0.18) * array
    return jnp.clip(array, min=-most, max=most).astype(kind)


def setup_inputs(seed: int = 0) -> dict:
    key_of = jax.random.split(jax.random.key(seed), 10)
    tokens = centred(key_of[0], (SEQS, WIN, D), 1.0, 6.0, ((0, 4), (1, 8)))
    lengths = draw_lengths(jax.random.fold_in(key_of[9], 71), 0)
    w_qkv = centred(key_of[2], (3, D, D), D ** -0.5, 0.1875, ((1, 4), (2, 8)))
    w_out = centred(key_of[3], (D, D), (D * 256 // WIN) ** -0.5, 0.75, ((0, 8), (1, 4)))
    w_fc = centred(key_of[4], (D, FF), D ** -0.5, 0.1875, ((0, 4), (1, 8)))
    w_proj = centred(key_of[5], (FF, D), FF ** -0.5, 0.09375, ((0, 8), (1, 4)))
    norm_gain = jnp.clip(1.0 + 0.18 * jax.random.normal(key_of[6], (2, D), jnp.float32), 0.1, 1.9)
    norm_bias = centred(key_of[7], (2, D), 0.5, 3.0, ((1, 32),), jnp.float32)
    cotangent = centred(key_of[8], (SEQS, WIN, D), 1.0, 6.0, ((0, 4), (1, 8)))
    return dict(tokens=tokens, lengths=lengths, w_qkv=w_qkv, w_out=w_out, w_fc=w_fc, w_proj=w_proj, norm_gain=norm_gain, norm_bias=norm_bias, cotangent=cotangent)


@jax.custom_vjp
def low(v):
    return lax.optimization_barrier(v.astype(jnp.bfloat16)).astype(jnp.float32)

@jax.custom_vjp
def low_back(v):
    return v

def low_keep(v):
    return (low(v), None)

def low_pass(kept, grad):
    return (grad,)

def back_keep(v):
    return (v, None)

def back_low(kept, grad):
    return (low(grad),)
low.defvjp(low_keep, low_pass)
low_back.defvjp(back_keep, back_low)
epsilon = 1e-05

def layer_norm(values, gain_row, bias_row):
    center = values - lax.optimization_barrier(jnp.mean(values, axis=-1, keepdims=True))
    spread = lax.optimization_barrier(jnp.mean(center * center, axis=-1, keepdims=True))
    return center * lax.rsqrt(spread + epsilon) * gain_row + bias_row

def window_attention(packed):
    proj_qkv, length = packed
    blocks = WIN // BLOCK
    shaped = proj_qkv.reshape(blocks, BLOCK, 3, HEADS, HEAD)
    queries = shaped[:, :, 0]
    key_rows = shaped[:, :, 1]
    value_rows = shaped[:, :, 2]
    raw = jnp.einsum('rchd,schd->chrs', queries, key_rows, precision=lax.Precision.HIGHEST) * HEAD ** (-0.5)
    scores = low_back(raw)
    column = lax.broadcasted_iota(jnp.int32, (BLOCK, 1, blocks, blocks), 0)
    query_row = lax.broadcasted_iota(jnp.int32, (BLOCK, 1, blocks, blocks), 2)
    key_row = lax.broadcasted_iota(jnp.int32, (BLOCK, 1, blocks, blocks), 3)
    allowed = (key_row <= query_row) & (key_row * BLOCK + column < length)
    probs = low(jax.nn.softmax(jnp.where(allowed, scores, -1e+30), axis=-1))
    mixed = jnp.einsum('chrs,schd->rchd', probs, value_rows, precision=lax.Precision.HIGHEST)
    return mixed.reshape(WIN, HEADS * HEAD)

def reference(tokens, lengths, w_qkv, w_out, w_fc, w_proj, norm_gain, norm_bias, cotangent):
    highest = lax.Precision.HIGHEST

    def forward(inputs, qkv_w, out_w, fc_w, proj_w, gains, biases):
        flat = inputs.reshape(SEQS * WIN, D)
        normed_one = low(layer_norm(flat, gains[0], biases[0]))
        proj_qkv = low_back(low(jnp.einsum('td,jde->tje', normed_one, qkv_w, precision=highest)))
        mixed = lax.map(jax.checkpoint(window_attention), (proj_qkv.reshape(SEQS, WIN, 3 * D), lengths))
        mixed = low_back(low(mixed.reshape(SEQS * WIN, D)))
        hidden = flat + low_back(jnp.dot(mixed, out_w, precision=highest))
        normed_two = low(layer_norm(hidden, gains[1], biases[1]))
        pre_act = low_back(jnp.dot(normed_two, fc_w, precision=highest))
        act_low = low(jax.nn.gelu(pre_act))
        output = hidden + jnp.dot(act_low, proj_w, precision=highest)
        return output.reshape(SEQS, WIN, D)
    floats = (tokens.astype(jnp.float32), w_qkv.astype(jnp.float32), w_out.astype(jnp.float32), w_fc.astype(jnp.float32), w_proj.astype(jnp.float32), norm_gain, norm_bias)
    output, pull = jax.vjp(forward, *floats)
    position = jnp.arange(WIN, dtype=jnp.int32)[None, :]
    is_valid = position < lengths[:, None]
    grads = pull(jnp.where(is_valid[:, :, None], cotangent.astype(jnp.float32), jnp.float32(0.0)))
    return (output.astype(jnp.bfloat16), grads[0].astype(jnp.bfloat16), grads[1], grads[2], grads[3], grads[4], grads[5], grads[6])
```

```python
import functools

import jax
import jax.numpy as jnp
from jax import lax
from jax.experimental import pallas as pl
from jax.experimental.pallas import tpu as pltpu
from jax.sharding import PartitionSpec as P

HEAD = 64
BLOCK = 128
COLS = 8
epsilon = 1e-05


def layer_norm(values, gain_row, bias_row):
    center = values - jnp.mean(values, axis=-1, keepdims=True)
    spread = jnp.mean(center * center, axis=-1, keepdims=True)
    return center * lax.rsqrt(spread + epsilon) * gain_row + bias_row


def swap(value, bits):
    size = lax.axis_size("tp")
    return lax.ppermute(value, "tp", [(i, i ^ bits) for i in range(size)])


def ring(value, step):
    size = lax.axis_size("sp")
    return lax.ppermute(value, "sp", [(i, (i + step) % size) for i in range(size)])


def gather_chips(own, chips):
    if chips != 4:
        return [own] + [swap(own, 2 * s) for s in range(1, chips)]
    from_x = swap(own, 2)
    from_y = swap(own, 4)
    far_low = swap(from_x[0], 4)
    far_high = swap(from_y[1], 2)
    return [own, from_x, from_y, jnp.stack([far_low, far_high])]


def scatter_chips(parts, chips):
    f32 = lambda v: v.astype(jnp.float32)
    if chips != 4:
        sums = [f32(v) for v in parts[0]]
        for s in range(1, chips):
            sums = [a + f32(swap(v, 2 * s)) for a, v in zip(sums, parts[s])]
        return sums
    low, high = 0, 1
    far_low = swap(parts[3][low], 2)
    far_high = swap(parts[3][high], 4)
    x_low = swap(parts[1][low], 2)
    y_high = swap(parts[2][high], 4)
    x_high = swap((f32(parts[1][high]) + f32(far_high)).astype(jnp.bfloat16), 2)
    y_low = swap((f32(parts[2][low]) + f32(far_low)).astype(jnp.bfloat16), 4)
    return [
        f32(parts[0][low]) + f32(x_low) + f32(y_low),
        f32(parts[0][high]) + f32(x_high) + f32(y_high),
    ]


def gather_rows(rows):
    count = lax.axis_size("sp")
    place = lax.axis_index("sp")
    pieces = jnp.stack([rows] + [ring(rows, step) for step in range(1, count)])
    pieces = pieces[(place - jnp.arange(count)) % count]
    whole = pieces.transpose(1, 0, 2).reshape(rows.shape[0], -1)
    bit, index = 1, lax.axis_index("tp")
    while bit < lax.axis_size("tp"):
        other = swap(whole, bit)
        upper = (index & bit) != 0
        whole = jnp.where(
            upper,
            jnp.concatenate([other, whole], axis=1),
            jnp.concatenate([whole, other], axis=1),
        )
        bit *= 2
    return whole


def scatter_rows(whole):
    index = lax.axis_index("tp")
    bit = lax.axis_size("tp") // 2
    while bit:
        half = whole.shape[1] // 2
        upper = (index & bit) != 0
        low, high = whole[:, :half], whole[:, half:]
        other = swap(jnp.where(upper, low, high), bit)
        whole = jnp.where(upper, high, low) + other
        bit //= 2
    count = lax.axis_size("sp")
    place = lax.axis_index("sp")
    parts = whole.reshape(whole.shape[0], count, -1)
    pick = lambda j: lax.dynamic_index_in_dim(parts, j % count, 1, keepdims=False)
    total = pick(place)
    for step in range(1, count):
        total = total + ring(pick(place + step), step)
    return total


def log2(n):
    assert n & (n - 1) == 0
    return n.bit_length() - 1


def allowed_mask(info, rows, chips, per):
    chip, core, length, first = info[0], info[1], info[2], info[3]

    def block_row(i):
        n = i >> log2(COLS)
        b = n & (per - 1)
        p = (n >> log2(per)) & (chips - 1)
        c = n >> log2(per * chips)
        return (((p ^ chip) * 2) + (c ^ core)) * per + b

    i = lax.broadcasted_iota(jnp.int32, (rows, rows), 0)
    j = lax.broadcasted_iota(jnp.int32, (rows, rows), 1)
    col = (j & (COLS - 1)) + first + pl.program_id(0) * COLS
    key_row = block_row(j)
    same = ((i ^ j) & (COLS - 1)) == 0
    return same & (key_row <= block_row(i)) & (key_row * BLOCK + col < length)


def dot(a, b, ca, cb):
    return lax.dot_general(a, b, (((ca,), (cb,)), ((), ())), preferred_element_type=jnp.float32)


def softmax_probs(q, k, allowed):
    scores = dot(q, k, 1, 1) * HEAD ** (-0.5)
    scores = jnp.where(allowed, scores, -1e30)
    e = jnp.exp(scores - jnp.max(scores, axis=-1, keepdims=True))
    return e / jnp.sum(e, axis=-1, keepdims=True)


def forward_kernel(info, qkv, out, *, chips, per):
    rows, width = out.shape[0] * out.shape[2], out.shape[3]
    allowed = allowed_mask(info, rows, chips, per)
    first = lax.broadcasted_iota(jnp.int32, (rows, 2 * HEAD), 1) < HEAD

    def load(ref, at):
        return ref[:, 0, :, at : at + 2 * HEAD].reshape(rows, 2 * HEAD)

    for at in range(0, width, 2 * HEAD):
        q, k, v = load(qkv, at), load(qkv, width + at), load(qkv, 2 * width + at)
        mixed = []
        for side in (first, ~first):
            probs = softmax_probs(jnp.where(side, q, jnp.zeros_like(q)), k, allowed)
            mixed.append(dot(probs.astype(jnp.bfloat16), v, 1, 0))
        both = jnp.where(first, mixed[0], mixed[1]).astype(out.dtype)
        out[:, 0, :, at : at + 2 * HEAD] = both.reshape(out.shape[0], out.shape[2], 2 * HEAD)


def backward_kernel(info, qkv, grad, out, *, chips, per):
    rows, width = grad.shape[0] * grad.shape[2], grad.shape[3]
    allowed = allowed_mask(info, rows, chips, per)
    first = lax.broadcasted_iota(jnp.int32, (rows, 2 * HEAD), 1) < HEAD

    def load(ref, at):
        return ref[:, 0, :, at : at + 2 * HEAD].reshape(rows, 2 * HEAD)

    for at in range(0, width, 2 * HEAD):
        q, k, v = load(qkv, at), load(qkv, width + at), load(qkv, 2 * width + at)
        g = load(grad, at)
        grads = []
        for side in (first, ~first):
            probs = softmax_probs(jnp.where(side, q, jnp.zeros_like(q)), k, allowed)
            grad_probs = dot(jnp.where(side, g, jnp.zeros_like(g)), v, 1, 1)
            along = jnp.sum(probs * grad_probs, axis=-1, keepdims=True)
            grad_scores = (probs * (grad_probs - along)).astype(jnp.bfloat16)
            grads.append(
                (
                    dot(grad_scores, k, 1, 0) * HEAD ** (-0.5),
                    dot(grad_scores, q, 0, 0) * HEAD ** (-0.5),
                    dot(probs.astype(jnp.bfloat16), g, 0, 0),
                )
            )
        for j in range(3):
            both = jnp.where(first, grads[0][j], grads[1][j]).astype(out.dtype)
            spot = j * width + at
            out[:, 0, :, spot : spot + 2 * HEAD] = both.reshape(
                out.shape[0], out.shape[2], 2 * HEAD
            )


def attention(kernel, info, operands, out_width, groups, chips, per, name):
    total = operands[0].shape[0]
    rows = total // (2 * groups)
    shaped = [v.reshape(2, groups, rows, v.shape[1]) for v in operands]
    spec = lambda width: pl.BlockSpec((2, 1, rows, width), lambda g, s: (0, g, 0, 0))
    return pl.pallas_call(
        functools.partial(kernel, chips=chips, per=per),
        grid_spec=pltpu.PrefetchScalarGridSpec(
            num_scalar_prefetch=1,
            grid=(groups,),
            in_specs=[spec(v.shape[1]) for v in operands],
            out_specs=spec(out_width),
        ),
        out_shape=jax.ShapeDtypeStruct((2, groups, rows, out_width), jnp.bfloat16),
        name=name,
    )(info, *shaped).reshape(total, out_width)


def mm(a, b, ca, cb):
    return dot(a, b, ca, cb)


def local(tokens, lengths, w_qkv, w_out, w_fc, w_proj, norm_gain, norm_bias, cotangent):
    bf16, f32 = jnp.bfloat16, jnp.float32
    tp = lax.axis_size("tp")
    chips = tp // 2
    index = lax.axis_index("tp")
    chip, core = index // 2, index % 2
    rows_own, width = tokens.shape[1:]
    per = rows_own // BLOCK
    groups = BLOCK // chips // COLS
    length = lengths[0]
    info = jnp.stack([chip, core, length, chip * (groups * COLS)]).astype(jnp.int32)

    def to_columns(rows):
        view = rows.reshape(per, chips, groups, COLS, width)
        pieces = []
        for s in range(chips):
            piece = lax.dynamic_index_in_dim(view, chip ^ s, 1, keepdims=False)
            piece = piece.transpose(1, 0, 2, 3)
            pieces.append(piece if s == 0 else swap(piece, 2 * s))
        return jnp.stack(pieces, axis=1).reshape(rows_own, width)

    def to_rows(cols):
        view = cols.reshape(groups, chips, per, COLS, width)
        out = jnp.zeros((per, chips, groups, COLS, width), cols.dtype)
        for s in range(chips):
            piece = view[:, s].transpose(1, 0, 2, 3)
            piece = piece if s == 0 else swap(piece, 2 * s)
            out = lax.dynamic_update_index_in_dim(out, piece, chip ^ s, 1)
        return out.reshape(tokens.shape)

    def both(mine):
        return jnp.concatenate([mine, swap(mine, 1)], axis=0)

    def share(partial):
        return partial[:rows_own] + swap(partial[rows_own:].astype(bf16), 1).astype(f32)

    qkv_z = lax.all_gather(w_qkv, "sp", axis=1, tiled=True)
    out_z = lax.all_gather(w_out, "sp", axis=1, tiled=True)
    fc_z = lax.all_gather(w_fc, "sp", axis=0, tiled=True)
    proj_z = lax.all_gather(w_proj, "sp", axis=1, tiled=True)
    part = w_qkv.shape[2]
    hidden_part = w_fc.shape[1]
    qkv_blocks = gather_chips(
        qkv_z.transpose(1, 0, 2).reshape(2, width // 2, 3 * part), chips
    )
    out_blocks = gather_chips(out_z.reshape(2, part // 2, width), chips)
    fc_blocks = gather_chips(fc_z.reshape(2, width // 2, hidden_part), chips)
    proj_blocks = gather_chips(proj_z.reshape(2, hidden_part // 2, width), chips)
    heads_width = chips * part
    qkv_w = jnp.stack([b.reshape(width, 3, part) for b in qkv_blocks], axis=2)
    qkv_w = qkv_w.reshape(width, 3 * heads_width)
    out_w = jnp.concatenate([b.reshape(part, width) for b in out_blocks], axis=0)
    fc_w = jnp.concatenate([b.reshape(width, hidden_part) for b in fc_blocks], axis=1)
    proj_w = jnp.concatenate([b.reshape(hidden_part, width) for b in proj_blocks], axis=0)

    norms = gather_rows(jnp.concatenate([norm_gain, norm_bias], axis=0))
    gains, biases = norms[:2], norms[2:]

    slot = lax.broadcasted_iota(jnp.int32, (groups, chips, per, COLS), 1)
    at = lax.broadcasted_iota(jnp.int32, (groups, chips, per, COLS), 2)
    group = lax.broadcasted_iota(jnp.int32, (groups, chips, per, COLS), 0)
    col = lax.broadcasted_iota(jnp.int32, (groups, chips, per, COLS), 3)
    block_row = ((slot ^ chip) * 2 + core) * per + at
    position = block_row * BLOCK + chip * (groups * COLS) + group * COLS + col
    is_valid = (position < length).reshape(rows_own, 1)

    inputs = to_columns(tokens[0]).astype(f32)
    normed_one, norm_one_pull = jax.vjp(layer_norm, inputs, gains[0], biases[0])
    ready_one = both(normed_one.astype(bf16))
    qkv = mm(ready_one, qkv_w, 1, 0).astype(bf16)
    mixed = attention(
        forward_kernel, info, [qkv], heads_width, groups, chips, per, "attention_forward"
    )
    hidden = inputs + share(mm(mixed, out_w, 1, 0))
    normed_two, norm_two_pull = jax.vjp(layer_norm, hidden, gains[1], biases[1])
    ready_two = both(normed_two.astype(bf16))

    grad_own = to_columns(cotangent[0])
    grad_own = jnp.where(is_valid, grad_own, jnp.zeros_like(grad_own))
    grad_all = both(grad_own)

    pre_act = mm(ready_two, fc_w, 1, 0)
    act_out, gelu_pull = jax.vjp(jax.nn.gelu, pre_act)
    slope = gelu_pull(jnp.ones_like(pre_act))[0].astype(bf16)
    act = act_out.astype(bf16)

    def blocks_of(left, right, on_right):
        out = []
        for s in range(chips):
            if on_right:
                n = right.shape[1] // chips
                block = mm(left, right[:, s * n : (s + 1) * n], 0, 0)
            else:
                n = left.shape[1] // chips
                block = mm(left[:, s * n : (s + 1) * n], right, 0, 0)
            block = block.astype(bf16)
            half = block.shape[0] // 2
            out.append((block[:half], block[half:]))
        return out

    proj_parts = blocks_of(act, grad_all, False)
    proj_sum = jnp.concatenate(scatter_chips(proj_parts, chips)).astype(bf16)
    output = (hidden + share(mm(act, proj_w, 1, 0))).astype(bf16)
    result = to_rows(output)

    grad_pre = (mm(grad_all, proj_w, 1, 1) * slope.astype(f32)).astype(bf16)
    fc_parts = blocks_of(ready_two, grad_pre, True)
    fc_sum = jnp.concatenate(scatter_chips(fc_parts, chips)).astype(bf16)
    grad_two = share(mm(grad_pre, fc_w, 1, 1))
    grad_h_norm, gain_two, bias_two = norm_two_pull(grad_two)
    grad_hidden = grad_own.astype(f32) + grad_h_norm
    branch = both(grad_hidden.astype(bf16))
    out_parts = blocks_of(mixed, branch, False)
    out_sum = jnp.concatenate(scatter_chips(out_parts, chips)).astype(bf16)
    grad_mixed = mm(branch, out_w, 1, 1).astype(bf16)
    grad_rows = attention(
        backward_kernel,
        info,
        [qkv, grad_mixed],
        3 * heads_width,
        groups,
        chips,
        per,
        "attention_backward",
    )
    rows_split = grad_rows.reshape(-1, 3, chips, part)
    qkv_parts = []
    for s in range(chips):
        block = mm(ready_one, rows_split[:, :, s].reshape(-1, 3 * part), 0, 0).astype(bf16)
        qkv_parts.append((block[: width // 2], block[width // 2 :]))
    qkv_sum = jnp.concatenate(scatter_chips(qkv_parts, chips)).astype(bf16)
    qkv_sum = qkv_sum.reshape(width, 3, part).transpose(1, 0, 2)
    grad_one = share(mm(grad_rows, qkv_w, 1, 1))
    grad_in_norm, gain_one, bias_one = norm_one_pull(grad_one)
    grad_inputs = to_rows((grad_hidden + grad_in_norm).astype(bf16))

    def over_windows(value, axis):
        return lax.psum_scatter(value, "sp", scatter_dimension=axis, tiled=True).astype(f32)

    norm_sums = scatter_rows(jnp.stack([gain_one, gain_two, bias_one, bias_two]))
    return (
        result,
        grad_inputs,
        over_windows(qkv_sum, 1),
        over_windows(out_sum, 1),
        over_windows(fc_sum, 0),
        over_windows(proj_sum, 1),
        norm_sums[:2],
        norm_sums[2:],
    )


def solution(mesh):
    in_specs = (
        P("sp", "tp", None),
        P("sp"),
        P(None, "sp", "tp"),
        P("tp", "sp"),
        P("sp", "tp"),
        P("tp", "sp"),
        P(None, ("tp", "sp")),
        P(None, ("tp", "sp")),
        P("sp", "tp", None),
    )
    out_specs = (
        P("sp", "tp", None),
        P("sp", "tp", None),
        P(None, "sp", "tp"),
        P("tp", "sp"),
        P("sp", "tp"),
        P("tp", "sp"),
        P(None, ("tp", "sp")),
        P(None, ("tp", "sp")),
    )
    return jax.shard_map(local, mesh=mesh, in_specs=in_specs, out_specs=out_specs, check_vma=False)
```

```python
import functools

import jax
import jax.numpy as jnp
from jax import lax
from jax.experimental import pallas as pl
from jax.experimental.pallas import tpu as pltpu
from jax.sharding import PartitionSpec as P

HEAD = 64
BLOCK = 128
COLS = 8
UNITS = 256
epsilon = 1e-05
bf16, f32 = jnp.bfloat16, jnp.float32


def layer_norm(values, gain_row, bias_row):
    center = values - jnp.mean(values, axis=-1, keepdims=True)
    spread = jnp.mean(center * center, axis=-1, keepdims=True)
    return center * lax.rsqrt(spread + epsilon) * gain_row + bias_row


def swap(value, bits, axis="tp"):
    size = lax.axis_size(axis)
    return lax.ppermute(value, axis, [(i, i ^ bits) for i in range(size)])


def log2(n):
    assert n & (n - 1) == 0
    return n.bit_length() - 1


def gather_windows(own):
    count = lax.axis_size("sp")
    pieces = {0: own}
    bit = count // 2
    while bit:
        pieces.update({k | bit: swap(v, bit, "sp") for k, v in list(pieces.items())})
        bit //= 2
    place = lax.axis_index("sp").astype(jnp.int32).reshape(1)
    zeros = (0,) * own.ndim

    def kernel(place, *refs):
        for k in range(count):
            pl.when(pl.program_id(0) == k)(lambda k=k: refs[-1].__setitem__(0, refs[k][...]))

    return pl.pallas_call(
        kernel,
        grid_spec=pltpu.PrefetchScalarGridSpec(
            num_scalar_prefetch=1,
            grid=(count,),
            in_specs=[pl.BlockSpec(own.shape, lambda k, z: zeros)] * count,
            out_specs=pl.BlockSpec((1, *own.shape), lambda k, z: (k ^ z[0], *zeros)),
        ),
        out_shape=jax.ShapeDtypeStruct((count, *own.shape), own.dtype),
        name="in_order",
    )(place, *[pieces[k] for k in range(count)])


def gather_chips(own, chips, via):
    if chips != 4:
        return [own] + [swap(own, 2 * s) for s in range(1, chips)]
    a, b = (2, 4) if via == 0 else (4, 2)
    got = {0: own, a // 2: swap(own, a), b // 2: swap(own, b)}
    got[3] = swap(got[b // 2], a)
    return [got[s] for s in range(4)]


def scatter_chips(parts, chips, via):
    if chips != 4:
        return [parts[0]] + [swap(parts[s], 2 * s) for s in range(1, chips)]
    a, b = (2, 4) if via == 0 else (4, 2)
    far = swap(parts[3], a)
    near = swap(parts[a // 2], a)
    relay = (parts[b // 2].astype(f32) + far.astype(f32)).astype(bf16)
    return [parts[0], near, swap(relay, b)]


def scatter_windows(terms):
    count = lax.axis_size("sp")
    place = lax.axis_index("sp")

    def piece(k):
        at = [lax.dynamic_index_in_dim(t, place ^ k, 0, keepdims=False) for t in terms]
        return sum(v.astype(f32) for v in at)

    held = {k: piece(k) for k in range(count)}
    bit = 1
    while bit < count:
        sent = [k for k in held if k & bit]
        got = swap(jnp.stack([held[k] for k in sent]).astype(bf16), bit, "sp")
        held = {k ^ bit: held[k ^ bit] + got[i].astype(f32) for i, k in enumerate(sent)}
        bit *= 2
    return held[0]


def gather_rows(rows):
    for axis in ("sp", "tp"):
        bit, index = 1, lax.axis_index(axis)
        while bit < lax.axis_size(axis):
            other = swap(rows, bit, axis)
            upper = (index & bit) != 0
            rows = jnp.concatenate(
                [jnp.where(upper, other, rows), jnp.where(upper, rows, other)], axis=1
            )
            bit *= 2
    return rows


def scatter_rows(whole):
    for axis in ("tp", "sp"):
        index = lax.axis_index(axis)
        bit = lax.axis_size(axis) // 2
        while bit:
            half = whole.shape[1] // 2
            upper = (index & bit) != 0
            low, high = whole[:, :half], whole[:, half:]
            other = swap(jnp.where(upper, low, high), bit, axis)
            whole = jnp.where(upper, high, low) + other
            bit //= 2
    return whole


def dot(a, b, ca, cb):
    return lax.dot_general(a, b, (((ca,), (cb,)), ((), ())), preferred_element_type=f32)


def whole_spec(v):
    zeros = (0,) * v.ndim
    return pl.BlockSpec(v.shape, lambda *_: zeros)


def call(kernel, grid, inputs, outputs, name, scalars=None, scratch=()):
    scalars = jnp.zeros((1,), jnp.int32) if scalars is None else scalars
    return pl.pallas_call(
        kernel,
        grid_spec=pltpu.PrefetchScalarGridSpec(
            num_scalar_prefetch=1,
            grid=grid,
            in_specs=[s for _, s in inputs],
            out_specs=[s for _, _, s in outputs],
            scratch_shapes=scratch,
        ),
        out_shape=[jax.ShapeDtypeStruct(s, d) for s, d, _ in outputs],
        name=name,
    )(scalars, *[v for v, _ in inputs])


def allowed_mask(info, rows, chips, per):
    chip, core, length, first = info[0], info[1], info[2], info[3]

    def block_row(i):
        n = i >> log2(COLS)
        b = n & (per - 1)
        p = (n >> log2(per)) & (chips - 1)
        c = n >> log2(per * chips)
        return (((p ^ chip) * 2) + (c ^ core)) * per + b

    i = lax.broadcasted_iota(jnp.int32, (rows, rows), 0)
    j = lax.broadcasted_iota(jnp.int32, (rows, rows), 1)
    col = (j & (COLS - 1)) + first + pl.program_id(0) * COLS
    key_row = block_row(j)
    same = ((i ^ j) & (COLS - 1)) == 0
    return same & (key_row <= block_row(i)) & (key_row * BLOCK + col < length)


def softmax_probs(q, k, allowed):
    scores = dot(q, k, 1, 1) * HEAD ** (-0.5)
    scores = jnp.where(allowed, scores, -1e30)
    e = jnp.exp(scores - jnp.max(scores, axis=-1, keepdims=True))
    return e / jnp.sum(e, axis=-1, keepdims=True)


def attention_kernel(info, own, other, *refs, chips, per, part):
    qkv_parts, out_parts = refs[:chips], refs[chips : 2 * chips]
    qkv_out, mixed_out, sum_own, sum_other, qkv_w, out_w = refs[2 * chips :]
    width = chips * part

    @pl.when(pl.program_id(0) == 0)
    def _():
        for s in range(chips):
            count, _, depth, _ = qkv_parts[s].shape
            wide = out_parts[s].shape[2]
            for z in range(count):
                for j in range(3):
                    at = j * width + s * part
                    qkv_w[z * depth : (z + 1) * depth, at : at + part] = qkv_parts[s][z, j]
                out_w[s * part : (s + 1) * part, z * wide : (z + 1) * wide] = out_parts[s][z]

    half = own.shape[0]
    rows = jnp.concatenate([own[...], other[...]], axis=0)
    qkv = dot(rows, qkv_w[...], 1, 0).astype(bf16)
    qkv_out[0], qkv_out[1] = qkv[:half], qkv[half:]
    allowed = allowed_mask(info, 2 * half, chips, per)
    first = lax.broadcasted_iota(jnp.int32, (2 * half, 2 * HEAD), 1) < HEAD
    for at in range(0, width, 2 * HEAD):
        q, k, v = (qkv[:, j * width + at : j * width + at + 2 * HEAD] for j in range(3))
        mixed = []
        for side in (first, ~first):
            probs = softmax_probs(jnp.where(side, q, jnp.zeros_like(q)), k, allowed)
            mixed.append(dot(probs.astype(bf16), v, 1, 0))
        pair = jnp.where(first, mixed[0], mixed[1]).astype(bf16)
        mixed_out[0, :, at : at + 2 * HEAD] = pair[:half]
        mixed_out[1, :, at : at + 2 * HEAD] = pair[half:]
    sum_own[...] = dot(mixed_out[0], out_w[...], 1, 0)
    sum_other[...] = dot(mixed_out[1], out_w[...], 1, 0).astype(bf16)


def attention_back_kernel(
    info, b_own, b_other, qkv, out_w, a_own, a_other, *refs, chips, per, part
):
    rows_out, parts, rows_all = refs[0], refs[1 : 1 + chips], refs[-1]
    half, width = b_own.shape[0], chips * part
    group = pl.program_id(0)
    branch = jnp.concatenate([b_own[...], b_other[...]], axis=0)
    grad_mixed = dot(branch, out_w[...], 1, 1).astype(bf16)
    allowed = allowed_mask(info, 2 * half, chips, per)
    first = lax.broadcasted_iota(jnp.int32, (2 * half, 2 * HEAD), 1) < HEAD
    for at in range(0, width, 2 * HEAD):
        q, k, v = (
            qkv[:, :, j * width + at : j * width + at + 2 * HEAD].reshape(2 * half, 2 * HEAD)
            for j in range(3)
        )
        g = grad_mixed[:, at : at + 2 * HEAD]
        grads = []
        for side in (first, ~first):
            probs = softmax_probs(jnp.where(side, q, jnp.zeros_like(q)), k, allowed)
            grad_probs = dot(jnp.where(side, g, jnp.zeros_like(g)), v, 1, 1)
            along = jnp.sum(probs * grad_probs, axis=-1, keepdims=True)
            grad_scores = (probs * (grad_probs - along)).astype(bf16)
            grads.append(
                (
                    dot(grad_scores, k, 1, 0) * HEAD ** (-0.5),
                    dot(grad_scores, q, 0, 0) * HEAD ** (-0.5),
                    dot(probs.astype(bf16), g, 0, 0),
                )
            )
        for j in range(3):
            pair = jnp.where(first, grads[0][j], grads[1][j]).astype(bf16)
            spot = j * width + at
            for c in range(2):
                mine = pair[c * half : (c + 1) * half]
                rows_out[c, :, spot : spot + 2 * HEAD] = mine
                rows_all[c, pl.ds(group * half, half), spot : spot + 2 * HEAD] = mine

    @pl.when(group == pl.num_programs(0) - 1)
    def _():
        for j in range(3):
            at = j * width
            block = dot(a_own[...], rows_all[0, :, at : at + width], 0, 0)
            block = block + dot(a_other[...], rows_all[1, :, at : at + width], 0, 0)
            block = block.astype(bf16)
            for s in range(chips):
                count, _, depth, _ = parts[s].shape
                for z in range(count):
                    parts[s][z, j] = block[z * depth : (z + 1) * depth, s * part : (s + 1) * part]


def out_grad_kernel(_, mixed, b_own, b_other, *parts):
    block = dot(mixed[0], b_own[...], 0, 0) + dot(mixed[1], b_other[...], 0, 0)
    block = block.astype(bf16)
    for s, ref in enumerate(parts):
        count, part, wide = ref.shape
        for z in range(count):
            ref[z] = block[s * part : (s + 1) * part, z * wide : (z + 1) * wide]


def pair_kernel(_, rows, weight, own, other, *, back):
    own[...] = dot(rows[0], weight[...], 1, 1 if back else 0)
    other[...] = dot(rows[1], weight[...], 1, 1 if back else 0).astype(bf16)


def pair_product(rows, weight, back, name):
    n, k = rows.shape[1:]
    m = weight.shape[0] if back else weight.shape[1]
    step = BLOCK
    out = pl.BlockSpec((step, m), lambda g, _: (g, 0))
    return call(
        functools.partial(pair_kernel, back=back),
        (n // step,),
        [(rows, pl.BlockSpec((2, step, k), lambda g, _: (0, g, 0))), (weight, whole_spec(weight))],
        [((n, m), f32, out), ((n, m), bf16, out)],
        name,
    )


def hidden_kernel(_, own, other, g_own, g_other, *refs, chips, steps):
    parts = refs[:chips]
    act_out, slope_out, fc_w = refs[chips : chips + 3]
    grads = refs[chips + 3 :]
    j = pl.program_id(0)
    for s in range(chips):

        @pl.when(j // steps == s)
        def _():
            count, depth, _ = parts[s].shape
            for z in range(count):
                fc_w[z * depth : (z + 1) * depth] = parts[s][z]

    scale = (2 / jnp.pi) ** 0.5
    for c, rows in enumerate((own, other)):
        u = dot(rows[...], fc_w[...], 1, 0)
        square = u * u
        t = jnp.tanh(scale * u * (1 + 0.044715 * square))
        act_out[c] = (0.5 * u * (1 + t)).astype(bf16)
        slope = 0.5 * (1 + t) + 0.5 * u * (1 - t * t) * scale * (1 + 3 * 0.044715 * square)
        slope_out[c] = slope.astype(bf16)
    block = dot(act_out[0], g_own[...], 0, 0) + dot(act_out[1], g_other[...], 0, 0)
    block = block.astype(bf16)
    for s in range(chips):

        @pl.when(j // steps == s)
        def _():
            count, _, wide = grads[s].shape
            for z in range(count):
                grads[s][z] = block[:, z * wide : (z + 1) * wide]


def hidden_back_kernel(_, g_own, g_other, own, other, slope, *refs, chips, steps):
    parts = refs[:chips]
    pre_out, proj_w = refs[chips : chips + 2]
    grads = refs[chips + 2 : -1]
    turned = refs[-1]
    j = pl.program_id(0)

    @pl.when(j == 0)
    def _():
        n = own.shape[0]
        turned[:, :n] = own[...].T
        turned[:, n:] = other[...].T

    for s in range(chips):

        @pl.when(j // steps == s)
        def _():
            count, _, wide = parts[s].shape
            for z in range(count):
                proj_w[:, z * wide : (z + 1) * wide] = parts[s][z]

    for c, g in enumerate((g_own, g_other)):
        grad_act = dot(g[...], proj_w[...], 1, 1)
        pre_out[c] = (grad_act * slope[c].astype(f32)).astype(bf16)
    pre = jnp.concatenate([pre_out[0], pre_out[1]], axis=0)
    block = dot(turned[...], pre, 1, 0).astype(bf16)
    for s in range(chips):

        @pl.when(j // steps == s)
        def _():
            count, depth, _ = grads[s].shape
            for z in range(count):
                grads[s][z] = block[z * depth : (z + 1) * depth]


def local(tokens, lengths, w_qkv, w_out, w_fc, w_proj, norm_gain, norm_bias, cotangent):
    tp, sp = lax.axis_size("tp"), lax.axis_size("sp")
    chips = tp // 2
    index = lax.axis_index("tp")
    chip, core = index // 2, index % 2
    rows_own, width = tokens.shape[1:]
    per = rows_own // BLOCK
    groups = BLOCK // chips // COLS
    share_rows = rows_own // groups
    length = lengths[0]
    info = jnp.stack([chip, core, length, chip * (groups * COLS)]).astype(jnp.int32)

    def to_columns(rows):
        view = rows.reshape(per, chips, groups, COLS, width)
        pieces = []
        for s in range(chips):
            piece = lax.dynamic_index_in_dim(view, chip ^ s, 1, keepdims=False)
            piece = piece.transpose(1, 0, 2, 3)
            pieces.append(piece if s == 0 else swap(piece, 2 * s))
        return jnp.stack(pieces, axis=1).reshape(rows_own, width)

    def to_rows(cols):
        view = cols.reshape(groups, chips, per, COLS, width)
        out = jnp.zeros((per, chips, groups, COLS, width), cols.dtype)
        for s in range(chips):
            piece = view[:, s].transpose(1, 0, 2, 3)
            piece = piece if s == 0 else swap(piece, 2 * s)
            out = lax.dynamic_update_index_in_dim(out, piece, chip ^ s, 1)
        return out.reshape(tokens.shape)

    def joined(sums):
        return sums[0] + swap(sums[1], 1).astype(f32)

    inputs = to_columns(tokens[0]).astype(f32)
    qkv_slots = gather_chips(gather_windows(w_qkv), chips, 0)
    out_slots = gather_chips(gather_windows(w_out), chips, 1)
    norms = gather_rows(jnp.concatenate([norm_gain, norm_bias], axis=0))
    gains, biases = norms[:2], norms[2:]
    fc_slots = gather_chips(gather_windows(w_fc), chips, 0)
    proj_slots = gather_chips(gather_windows(w_proj), chips, 1)
    part, hidden_part = w_qkv.shape[2], w_fc.shape[1]
    heads_width, hidden_width = chips * part, chips * hidden_part
    steps = hidden_part // UNITS

    shape = (groups, chips, per, COLS)
    group, slot, at, col = (lax.broadcasted_iota(jnp.int32, shape, i) for i in range(4))
    block_row = ((slot ^ chip) * 2 + core) * per + at
    position = block_row * BLOCK + chip * (groups * COLS) + group * COLS + col
    is_valid = (position < length).reshape(rows_own, 1)

    normed_one, norm_one_pull = jax.vjp(layer_norm, inputs, gains[0], biases[0])
    a_own = normed_one.astype(bf16)
    a_other = swap(a_own, 1)
    by_group = lambda w: pl.BlockSpec((share_rows, w), lambda g, _: (g, 0))
    by_group2 = lambda w: pl.BlockSpec((2, share_rows, w), lambda g, _: (0, g, 0))
    const = lambda *shape: pl.BlockSpec(shape, lambda *_: (0,) * len(shape))
    qkv, mixed, mix_own, mix_other, qkv_w, out_w = call(
        functools.partial(attention_kernel, chips=chips, per=per, part=part),
        (groups,),
        [(a_own, by_group(width)), (a_other, by_group(width))]
        + [(v, whole_spec(v)) for v in qkv_slots + out_slots],
        [
            ((2, rows_own, 3 * heads_width), bf16, by_group2(3 * heads_width)),
            ((2, rows_own, heads_width), bf16, by_group2(heads_width)),
            ((rows_own, width), f32, by_group(width)),
            ((rows_own, width), bf16, by_group(width)),
            ((width, 3 * heads_width), bf16, const(width, 3 * heads_width)),
            ((heads_width, width), bf16, const(heads_width, width)),
        ],
        "attention",
        info,
    )
    hidden = inputs + joined((mix_own, mix_other))
    normed_two, norm_two_pull = jax.vjp(layer_norm, hidden, gains[1], biases[1])
    n_own = normed_two.astype(bf16)
    n_other = swap(n_own, 1)

    grad_own = to_columns(cotangent[0])
    grad_own = jnp.where(is_valid, grad_own, jnp.zeros_like(grad_own))
    grad_other = swap(grad_own, 1)

    clip = lambda j, s: jnp.clip(j - s * steps, 0, steps - 1)
    depth, wide = width // sp, width // sp
    fc_spec = lambda s: pl.BlockSpec((sp, depth, UNITS), lambda j, _: (0, 0, clip(j, s)))
    proj_spec = lambda s: pl.BlockSpec((sp, UNITS, wide), lambda j, _: (0, clip(j, s), 0))
    units2 = pl.BlockSpec((2, rows_own, UNITS), lambda j, _: (0, 0, j))
    act, slope, fc_w, *proj_parts = call(
        functools.partial(hidden_kernel, chips=chips, steps=steps),
        (chips * steps,),
        [(v, whole_spec(v)) for v in (n_own, n_other, grad_own, grad_other)]
        + [(v, fc_spec(s)) for s, v in enumerate(fc_slots)],
        [
            ((2, rows_own, hidden_width), bf16, units2),
            ((2, rows_own, hidden_width), bf16, units2),
            ((width, hidden_width), bf16, pl.BlockSpec((width, UNITS), lambda j, _: (0, j))),
        ]
        + [((sp, hidden_part, wide), bf16, proj_spec(s)) for s in range(chips)],
        "hidden_forward",
    )
    proj_terms = scatter_chips(proj_parts, chips, 1)
    grad_pre, proj_w, *fc_parts = call(
        functools.partial(hidden_back_kernel, chips=chips, steps=steps),
        (chips * steps,),
        [(v, whole_spec(v)) for v in (grad_own, grad_other, n_own, n_other)]
        + [(slope, units2)]
        + [(v, proj_spec(s)) for s, v in enumerate(proj_slots)],
        [
            ((2, rows_own, hidden_width), bf16, units2),
            ((hidden_width, width), bf16, pl.BlockSpec((UNITS, width), lambda j, _: (j, 0))),
        ]
        + [((sp, depth, hidden_part), bf16, fc_spec(s)) for s in range(chips)],
        "hidden_backward",
        scratch=[pltpu.VMEM((width, 2 * rows_own), bf16)],
    )
    fc_terms = scatter_chips(fc_parts, chips, 0)
    output = (hidden + joined(pair_product(act, proj_w, False, "project"))).astype(bf16)
    result = to_rows(output)
    sum_proj = scatter_windows(proj_terms)

    grad_two = joined(pair_product(grad_pre, fc_w, True, "project_backward"))
    grad_h_norm, gain_two, bias_two = norm_two_pull(grad_two)
    grad_hidden = grad_own.astype(f32) + grad_h_norm
    b_own = grad_hidden.astype(bf16)
    b_other = swap(b_own, 1)
    out_parts = call(
        out_grad_kernel,
        (1,),
        [(v, whole_spec(v)) for v in (mixed, b_own, b_other)],
        [((sp, part, wide), bf16, const(sp, part, wide))] * chips,
        "out_gradient",
    )
    out_terms = scatter_chips(out_parts, chips, 1)
    grad_rows, *qkv_parts = call(
        functools.partial(attention_back_kernel, chips=chips, per=per, part=part),
        (groups,),
        [
            (b_own, by_group(width)),
            (b_other, by_group(width)),
            (qkv, by_group2(3 * heads_width)),
            (out_w, whole_spec(out_w)),
            (a_own, whole_spec(a_own)),
            (a_other, whole_spec(a_other)),
        ],
        [((2, rows_own, 3 * heads_width), bf16, by_group2(3 * heads_width))]
        + [((sp, 3, depth, part), bf16, const(sp, 3, depth, part))] * chips,
        "attention_backward",
        info,
        [pltpu.VMEM((2, rows_own, 3 * heads_width), bf16)],
    )
    qkv_terms = scatter_chips(qkv_parts, chips, 0)
    sum_fc = scatter_windows(fc_terms)
    sum_out = scatter_windows(out_terms)
    grad_one = joined(pair_product(grad_rows, qkv_w, True, "rows_backward"))
    grad_in_norm, gain_one, bias_one = norm_one_pull(grad_one)
    grad_inputs = to_rows((grad_hidden + grad_in_norm).astype(bf16))
    sum_qkv = scatter_windows(qkv_terms)
    norm_sums = scatter_rows(jnp.stack([gain_one, gain_two, bias_one, bias_two]))
    return (
        result,
        grad_inputs,
        sum_qkv,
        sum_out,
        sum_fc,
        sum_proj,
        norm_sums[:2],
        norm_sums[2:],
    )


def solution(mesh):
    in_specs = (
        P("sp", "tp", None),
        P("sp"),
        P(None, "sp", "tp"),
        P("tp", "sp"),
        P("sp", "tp"),
        P("tp", "sp"),
        P(None, ("tp", "sp")),
        P(None, ("tp", "sp")),
        P("sp", "tp", None),
    )
    out_specs = (
        P("sp", "tp", None),
        P("sp", "tp", None),
        P(None, "sp", "tp"),
        P("tp", "sp"),
        P("sp", "tp"),
        P("tp", "sp"),
        P(None, ("tp", "sp")),
        P(None, ("tp", "sp")),
    )
    return jax.shard_map(local, mesh=mesh, in_specs=in_specs, out_specs=out_specs, check_vma=False)
```
